768 devices in a mesh: dp: 48 (over y_lo, z), weight: 16 (over x, y_hi, core).
Axes of the slice: x: 4, y: 8 (y_hi: 2, y_lo: 4; y = y_hi * 4 + y_lo), z: 12, core: 2. Of those that a mesh axis runs over, the one named last changes fastest.
Arguments:
- tokens: bfloat16 [6144, 8192], P('dp'), may hold values from -6 to 6
- block_values: bfloat16 [16, 48, 128, 128], P('weight', 'dp'), may hold values from -0.4375 to 0.4375
- block_rows: int32 [16, 48], P('weight'), may hold values from 0 to 63, as said below
- block_cols: int32 [16, 48], P('weight'), may hold values from 0 to 15
- block_counts: int32 [16], P('weight'), may hold values from 1 to 48, as said below
- cotangent: bfloat16 [6144, 32768], P('dp', 'weight'), may hold values from -6 to 6
Outputs:
- activated: bfloat16 [6144, 32768], P('dp', 'weight')
- input_grad: bfloat16 [6144, 8192], P('dp', 'weight')
- block_grad: float32 [16, 48, 128, 128], P('weight', 'dp')
The draws below stay inside these ranges and needn't reach their ends.
Inputs may be any that keep to these rules, and one draw needn't show every extreme that they name: In each panel the 48 pairs (block_rows, block_cols) name distinct blocks. `block_counts`: some panel has all 48 slots live.
All inputs are finite; a program needn't handle non-finite values.
Results may differ from the reference program's by a relative error of at most 0.015.
Values may be sent and summed in bfloat16 or wider, within the bound.
A program may use at most 64 MiB of HBM per device.

```python
import math
import jax
import jax.numpy as jnp
from jax import lax

D = 8192
PW = 2048
PANELS = 16
SLOTS = 48
TOKENS = 6144
H = 32768


def mask_layout(key):
    grid_cells = D // 128 * (PW // 128)
    panel_keys = jax.random.split(jax.random.fold_in(key, 7), PANELS)
    chosen = jax.vmap(lambda one_key: jax.random.permutation(one_key, grid_cells)[:SLOTS])(panel_keys)
    chosen = chosen.astype(jnp.int32)
    return (chosen // (PW // 128), chosen % (PW // 128))


def draw_block_rows(key, part):
    return mask_layout(key)[0].astype(jnp.int32)


def draw_block_cols(key, part):
    return mask_layout(key)[1].astype(jnp.int32)


def draw_block_counts(key, part):
    drawn = jax.random.randint(jax.random.fold_in(key, 11), (PANELS,), 1, SLOTS + 1)
    fullest = jax.random.randint(jax.random.fold_in(key, 13), (), 0, PANELS)
    return jnp.where(jnp.arange(PANELS) == fullest, SLOTS, drawn).astype(jnp.int32)


def block_levels(key, extent, shards, smallest, largest):
    gain, own = 1.0, jax.random.fold_in(key, 6)
    for axis_at, shards_of in shards:
        heights = jnp.exp(jax.random.uniform(jax.random.fold_in(own, axis_at), (shards_of,), jnp.float32, smallest / len(shards), largest / len(shards)))
        gain = gain * jnp.repeat(heights, extent[axis_at] // shards_of).reshape([-1 if axis == axis_at else 1 for axis in range(len(extent))])
    return gain


def noise(own_key, dims, spread, most, pieces=(), kind=jnp.bfloat16):
    gain = block_levels(own_key, dims, pieces, -0.22, 0.18) if pieces else 1.0
    result = jax.random.normal(own_key, dims, jnp.float32) * spread * gain
    return jnp.minimum(jnp.maximum(result, -most), most).astype(kind)


def setup_inputs(seed: int = 0) -> dict:
    splits = jax.random.split(jax.random.key(seed), 7)
    tokens = noise(splits[0], (TOKENS, D), 1.0, 6.0, ((0, 48),))
    block_values = noise(splits[1], (PANELS, SLOTS, 128, 128), (SLOTS * 8192 // PW) ** -0.5, 0.4375, ((0, 16), (1, 48)))
    block_rows = draw_block_rows(jax.random.fold_in(splits[6], 71), 0)
    block_cols = draw_block_cols(jax.random.fold_in(splits[6], 71), 0)
    block_counts = draw_block_counts(jax.random.fold_in(splits[6], 71), 0)
    cotangent = noise(splits[5], (TOKENS, H), 1.0, 6.0, ((0, 48), (1, 16)))
    return {"tokens": tokens, "block_values": block_values, "block_rows": block_rows, "block_cols": block_cols, "block_counts": block_counts, "cotangent": cotangent}


def panel_work(tokens, panel_vals, slot_rows, slot_cols, live_count, cot_panel):
    tok_count = tokens.shape[0]
    blocked = tokens.reshape(tok_count, D // 128, 128)
    live_slots = (jnp.arange(SLOTS) < live_count).astype(jnp.float32)
    col_pick = (slot_cols[:, None] == jnp.arange(PW // 128)[None, :]).astype(jnp.float32) * live_slots[:, None]
    row_pick = (slot_rows[:, None] == jnp.arange(D // 128)[None, :]).astype(jnp.float32) * live_slots[:, None]
    picked = jnp.take(blocked, slot_rows, axis=1).astype(jnp.float32)
    blocks_f = panel_vals.astype(jnp.float32)
    contrib = jnp.einsum('tsk,skn->tsn', picked, blocks_f, precision=lax.Precision.HIGHEST)
    preact = jnp.einsum('tsn,sc->tcn', contrib, col_pick, precision=lax.Precision.HIGHEST).reshape(tok_count, PW)
    gate_sig = jax.nn.sigmoid(preact)
    activated = (preact * gate_sig).astype(jnp.bfloat16)
    grad_pre = (cot_panel.astype(jnp.float32) * gate_sig * (1.0 + preact * (1.0 - gate_sig))).astype(jnp.bfloat16)
    grad_slot = jnp.take(grad_pre.reshape(tok_count, PW // 128, 128), slot_cols, axis=1).astype(jnp.float32)
    block_grad = jnp.einsum('tsk,tsn->skn', picked, grad_slot, precision=lax.Precision.HIGHEST)
    block_grad = block_grad * live_slots[:, None, None] / math.sqrt(TOKENS)
    back_terms = jnp.einsum('tsn,skn->tsk', grad_slot, blocks_f, precision=lax.Precision.HIGHEST)
    partial_value = jnp.einsum('tsk,sr->trk', back_terms, row_pick, precision=lax.Precision.HIGHEST)
    partial_value = partial_value.reshape(tok_count, D).astype(jnp.bfloat16)
    return (activated, block_grad, partial_value)

def reference(tokens, block_values, block_rows, block_cols, block_counts, cotangent):
    cot_panels = jnp.transpose(cotangent.reshape(TOKENS, PANELS, PW), (1, 0, 2))

    def panel_step(grad_total, panel_item):
        panel_vals, slot_rows, slot_cols, live_count, cot_panel = panel_item
        activated, block_grad, partial_value = panel_work(tokens, panel_vals, slot_rows, slot_cols, live_count, cot_panel)
        return (grad_total + partial_value.astype(jnp.float32), (activated, block_grad))
    grad_total, (act_stack, grad_stack) = lax.scan(panel_step, jnp.zeros((TOKENS, D), jnp.float32), (block_values, block_rows, block_cols, block_counts, cot_panels))
    activated = jnp.transpose(act_stack, (1, 0, 2)).reshape(TOKENS, PANELS * PW)
    return (activated, grad_total.astype(jnp.bfloat16), grad_stack)
```

```python
import functools
import math

import jax
import jax.numpy as jnp
from jax import lax
from jax.experimental import pallas as pl
from jax.experimental.pallas import tpu as pltpu
from jax.sharding import PartitionSpec as P

MESH = pl.DeviceIdType.MESH
NY, NZ, NX = 4, 12, 4
F32, BF16 = jnp.float32, jnp.bfloat16


def mod(a, n):
    return lax.rem(a + n, n)


def hops(delta, side):
    long_way, short_way = NZ // 2, NZ - 1 - NZ // 2
    return long_way if (delta + side) % 2 == 0 else short_way


def greet(partners):
    barrier = pltpu.get_barrier_semaphore()
    for dp, weight in partners:
        pl.semaphore_signal(barrier, inc=1, device_id=(dp, weight), device_id_type=MESH)
    pl.semaphore_wait(barrier, len(partners))


def gather_kernel(own_ref, out_ref, own_sem, y_send, y_recv, z_send, z_recv):
    dp, weight = lax.axis_index("dp"), lax.axis_index("weight")
    j, z = dp // NZ, lax.rem(dp, NZ)
    sides = (mod(z + 1, NZ), mod(z - 1, NZ))
    greet(
        [(mod(j + delta, NY) * NZ + z, weight) for delta in range(1, NY)]
        + [(j * NZ + side, weight) for side in sides]
    )
    keep = pltpu.make_async_copy(own_ref, out_ref.at[dp], own_sem)
    keep.start()

    def y_copy(delta):
        return pltpu.make_async_remote_copy(
            src_ref=own_ref,
            dst_ref=out_ref.at[dp],
            send_sem=y_send.at[delta - 1],
            recv_sem=y_recv.at[delta - 1],
            device_id=(mod(j + delta, NY) * NZ + z, weight),
            device_id_type=MESH,
        )

    def z_copy(side, delta, step):
        back = -step if side == 0 else step
        slot = mod(j - delta, NY) * NZ + mod(z + back, NZ)
        return pltpu.make_async_remote_copy(
            src_ref=own_ref if (delta == 0 and step == 0) else out_ref.at[slot],
            dst_ref=out_ref.at[slot],
            send_sem=z_send.at[side, delta, step],
            recv_sem=z_recv.at[side, delta, step],
            device_id=(j * NZ + sides[side], weight),
            device_id_type=MESH,
        )

    started = []
    for side in range(2):
        copy = z_copy(side, 0, 0)
        copy.start()
        started.append(copy)
    for delta in range(1, NY):
        copy = y_copy(delta)
        copy.start()
        started.append(copy)
    for delta in range(1, NY):
        y_copy(delta).wait_recv()
        for side in range(2):
            copy = z_copy(side, delta, 0)
            copy.start()
            started.append(copy)
    for step in range(1, NZ // 2 + 1):
        for delta in range(NY):
            for side in range(2):
                if step > hops(delta, side):
                    continue
                z_copy(side, delta, step - 1).wait_recv()
                if step < hops(delta, side):
                    copy = z_copy(side, delta, step)
                    copy.start()
                    started.append(copy)
    for copy in started:
        copy.wait_send()
    keep.wait()


def gather_blocks(own, slots):
    size = own.shape
    return pl.pallas_call(
        gather_kernel,
        out_shape=jax.ShapeDtypeStruct((slots,) + size, own.dtype),
        in_specs=[pl.BlockSpec(memory_space=pltpu.VMEM)],
        out_specs=pl.BlockSpec(memory_space=pltpu.VMEM),
        scratch_shapes=[
            pltpu.SemaphoreType.DMA,
            pltpu.SemaphoreType.DMA((NY - 1,)),
            pltpu.SemaphoreType.DMA((NY - 1,)),
            pltpu.SemaphoreType.DMA((2, NY, NZ // 2)),
            pltpu.SemaphoreType.DMA((2, NY, NZ // 2)),
        ],
        compiler_params=pltpu.CompilerParams(collective_id=0, has_side_effects=True),
        name="gather_blocks",
    )(own)


UNROLL = 8


def local_kernel(
    rows_ref, cols_ref, count_ref, tokens_ref, blocks_ref, cot_ref,
    act_ref, back_ref, grads_ref, acc_ref, grad_pre_ref, back_acc_ref,
):
    slots = blocks_ref.shape[0]
    col_blocks = grad_pre_ref.shape[0]
    row_blocks = back_acc_ref.shape[0] - 1
    count = count_ref[0]
    acc_ref[...] = jnp.zeros_like(acc_ref)

    def picked(slot):
        return tokens_ref[:, pl.ds(pl.multiple_of(rows_ref[slot] * 128, 128), 128)]

    def forward(group, carry):
        for at in range(UNROLL):
            slot = group * UNROLL + at
            col = jnp.where(slot < count, cols_ref[slot], col_blocks)
            acc_ref[col] += jnp.dot(picked(slot), blocks_ref[slot], preferred_element_type=F32)
        return carry

    lax.fori_loop(0, slots // UNROLL, forward, 0)
    back_acc_ref[...] = jnp.zeros_like(back_acc_ref)
    for col in range(col_blocks):
        here = slice(col * 128, col * 128 + 128)
        preact = acc_ref[col]
        gate = jax.nn.sigmoid(preact)
        act_ref[:, here] = (preact * gate).astype(BF16)
        grad_pre_ref[col] = (
            cot_ref[:, here].astype(F32) * gate * (1.0 + preact * (1.0 - gate))
        ).astype(BF16)

    def backward(group, carry):
        for at in range(UNROLL):
            slot = group * UNROLL + at
            live = slot < count
            row = jnp.where(live, rows_ref[slot], row_blocks)
            grad = grad_pre_ref[cols_ref[slot]]
            back_acc_ref[row] += lax.dot_general(
                grad, blocks_ref[slot], (((1,), (1,)), ((), ())), preferred_element_type=F32
            )
            partial = lax.dot_general(
                picked(slot), grad, (((0,), (0,)), ((), ())), preferred_element_type=F32
            )
            grads_ref[slot] = (partial * live.astype(F32)).astype(BF16)
        return carry

    lax.fori_loop(0, slots // UNROLL, backward, 0)
    wide = back_ref.shape[2] // 128
    for row in range(row_blocks):
        at = (row % wide) * 128
        back_ref[row // wide, :, at:at + 128] = back_acc_ref[row].astype(BF16)


def local_work(rows, cols, count, tokens, blocks, cot, owners):
    tok, feat = tokens.shape
    slots = blocks.shape[0]
    panel = cot.shape[1]
    smem = pl.BlockSpec(memory_space=pltpu.SMEM)
    vmem = pl.BlockSpec(memory_space=pltpu.VMEM)
    return pl.pallas_call(
        local_kernel,
        out_shape=(
            jax.ShapeDtypeStruct((tok, panel), BF16),
            jax.ShapeDtypeStruct((owners, tok, feat // owners), BF16),
            jax.ShapeDtypeStruct((slots, 128, 128), BF16),
        ),
        in_specs=[smem, smem, smem, vmem, vmem, vmem],
        out_specs=(vmem, vmem, vmem),
        scratch_shapes=[
            pltpu.VMEM((panel // 128 + 1, tok, 128), F32),
            pltpu.VMEM((panel // 128, tok, 128), BF16),
            pltpu.VMEM((feat // 128 + 1, tok, 128), F32),
        ],
        compiler_params=pltpu.CompilerParams(vmem_limit_bytes=32 << 20),
        name="local_work",
    )(rows, cols, count, tokens, blocks, cot)


def reduce_kernel(
    scale, back_ref, grads_ref, in_grad_ref, block_grad_ref,
    z_buf, y_buf, y_out, c_buf, x_sum, x_buf, h_out, h_buf,
    z_send, z_recv, y_send, y_recv, c_send, c_recv, x_send, x_recv, h_send, h_recv,
):
    dp, weight = lax.axis_index("dp"), lax.axis_index("weight")
    j, z = dp // NZ, lax.rem(dp, NZ)
    x, h, core = weight // 4, lax.rem(weight // 2, 2), lax.rem(weight, 2)
    sides = (mod(z + 1, NZ), mod(z - 1, NZ))
    x_sides = (mod(x + 1, NX), mod(x - 1, NX))
    sibling = weight + 1 - 2 * core
    x_weight = [(side * 2 + h) * 2 + core for side in x_sides]
    h_weight = (x * 2 + 1 - h) * 2 + core
    greet(
        [(mod(j + delta, NY) * NZ + z, weight) for delta in range(1, NY)]
        + [(j * NZ + side, weight) for side in sides]
        + [(dp, sibling)]
        + [(dp, side) for side in x_weight]
        + [(dp, h_weight)]
    )
    started = []

    def go(copy):
        copy.start()
        started.append(copy)

    def send(src, dst, send_sem, recv_sem, device):
        return pltpu.make_async_remote_copy(
            src_ref=src, dst_ref=dst, send_sem=send_sem, recv_sem=recv_sem,
            device_id=device, device_id_type=MESH,
        )

    def z_slot(side, delta, step):
        ahead = hops(delta, side) - step
        return mod(j + delta, NY) * NZ + mod(z + (ahead if side == 0 else -ahead), NZ)

    def z_copy(side, delta, step):
        src = grads_ref.at[z_slot(side, delta, 0)] if step == 0 else z_buf.at[side, delta, step - 1]
        return send(
            src, z_buf.at[side, delta, step], z_send.at[side, delta, step],
            z_recv.at[side, delta, step], (j * NZ + sides[side], weight),
        )

    def z_step(step):
        for delta in range(NY):
            for side in range(2):
                if step >= hops(delta, side):
                    continue
                if step > 0:
                    z_copy(side, delta, step - 1).wait_recv()
                    z_buf[side, delta, step - 1] = (
                        z_buf[side, delta, step - 1].astype(F32)
                        + grads_ref[z_slot(side, delta, step)].astype(F32)
                    ).astype(BF16)
                go(z_copy(side, delta, step))

    def owner(dx, half, which):
        return (mod(x + dx, NX) * 2 + mod(h + half, 2)) * 2 + which

    def c_copy(dx, half):
        return send(
            back_ref.at[owner(dx, half, 1 - core)], c_buf.at[dx, half],
            c_send.at[dx, half], c_recv.at[dx, half], (dp, sibling),
        )

    def c_sum(dx, half):
        c_copy(dx, half).wait_recv()
        return c_buf[dx, half].astype(F32) + back_ref[owner(dx, half, core)].astype(F32)

    def x_copy(side, what):
        return send(
            x_sum.at[side, what], x_buf.at[side, what], x_send.at[side, what],
            x_recv.at[side, what], (dp, x_weight[side]),
        )

    def h_copy():
        return send(h_out, h_buf, h_send, h_recv, (dp, h_weight))

    order = [(2, 1), (2, 0), (3, 1), (1, 0), (1, 1), (3, 0), (0, 1), (0, 0)]
    for dx, half in order[:2]:
        go(c_copy(dx, half))
    z_step(0)
    for dx, half in order[2:]:
        go(c_copy(dx, half))
    for half, side in ((1, 0), (0, 1)):
        x_sum[side, 0] = c_sum(2, half).astype(BF16)
        go(x_copy(side, 0))
    for half, side, dx in ((1, 1, 3), (0, 0, 1)):
        x_sum[side, 1] = c_sum(dx, half).astype(BF16)
        go(x_copy(side, 1))
    z_step(1)
    for half, side, dx in ((1, 0, 1), (0, 1, 3)):
        own = c_sum(dx, half)
        x_copy(side, 0).wait_recv()
        x_sum[side, 2] = (own + x_buf[side, 0].astype(F32)).astype(BF16)
        go(x_copy(side, 2))
    z_step(2)
    total = c_sum(0, 1)
    x_copy(1, 1).wait_recv()
    total += x_buf[1, 1].astype(F32)
    z_step(3)
    x_copy(0, 2).wait_recv()
    h_out[...] = (total + x_buf[0, 2].astype(F32)).astype(BF16)
    go(h_copy())
    z_step(4)
    total = c_sum(0, 0)
    x_copy(0, 1).wait_recv()
    total += x_buf[0, 1].astype(F32)
    x_copy(1, 2).wait_recv()
    total += x_buf[1, 2].astype(F32)
    z_step(5)

    def z_total(delta):
        value = grads_ref[mod(j + delta, NY) * NZ + z].astype(F32)
        for side in range(2):
            last = hops(delta, side) - 1
            z_copy(side, delta, last).wait_recv()
            value += z_buf[side, delta, last].astype(F32)
        return value

    def y_copy(delta):
        return send(
            y_out.at[delta - 1], y_buf.at[delta - 1], y_send.at[delta - 1], y_recv.at[delta - 1],
            (mod(j + delta, NY) * NZ + z, weight),
        )

    for delta in (2, 1, 3):
        y_out[delta - 1] = z_total(delta).astype(BF16)
        go(y_copy(delta))
    grad = z_total(0)
    h_copy().wait_recv()
    in_grad_ref[...] = (total + h_buf[...].astype(F32)).astype(BF16)
    for delta in (2, 1, 3):
        y_copy(delta).wait_recv()
        grad += y_buf[delta - 1].astype(F32)
    block_grad_ref[...] = grad * scale
    for copy in started:
        copy.wait_send()


def reduce_all(back, grads, scale):
    owners, tok, width = back.shape
    vmem = pl.BlockSpec(memory_space=pltpu.VMEM)
    part = (tok, width)
    dma = pltpu.SemaphoreType.DMA
    return pl.pallas_call(
        functools.partial(reduce_kernel, scale),
        out_shape=(
            jax.ShapeDtypeStruct(part, BF16),
            jax.ShapeDtypeStruct(grads.shape[1:], F32),
        ),
        in_specs=[vmem, vmem],
        out_specs=(vmem, vmem),
        scratch_shapes=[
            pltpu.VMEM((2, NY, NZ // 2) + grads.shape[1:], BF16),
            pltpu.VMEM((NY - 1,) + grads.shape[1:], BF16),
            pltpu.VMEM((NY - 1,) + grads.shape[1:], BF16),
            pltpu.VMEM((NX, 2) + part, BF16),
            pltpu.VMEM((2, 3) + part, BF16),
            pltpu.VMEM((2, 3) + part, BF16),
            pltpu.VMEM(part, BF16),
            pltpu.VMEM(part, BF16),
            dma((2, NY, NZ // 2)),
            dma((2, NY, NZ // 2)),
            dma((NY - 1,)),
            dma((NY - 1,)),
            dma((NX, 2)),
            dma((NX, 2)),
            dma((2, 3)),
            dma((2, 3)),
            dma,
            dma,
        ],
        compiler_params=pltpu.CompilerParams(
            collective_id=1, has_side_effects=True, vmem_limit_bytes=32 << 20
        ),
        name="reduce_all",
    )(back, grads)


def local(tokens, block_values, block_rows, block_cols, block_counts, cotangent):
    owners = lax.axis_size("weight")
    blocks = gather_blocks(block_values[0, 0], block_rows.shape[1])
    activated, back, grads = local_work(
        block_rows[0], block_cols[0], block_counts, tokens, blocks, cotangent, owners
    )
    scale = 1.0 / math.sqrt(tokens.shape[0] * lax.axis_size("dp"))
    input_grad, block_grad = reduce_all(back, grads, scale)
    return (activated, input_grad, block_grad.reshape(block_values.shape))


def solution(mesh):
    placed = (
        P("dp", None),
        P("weight", "dp", None, None),
        P("weight", None),
        P("weight", None),
        P("weight"),
        P("dp", "weight"),
    )
    return jax.shard_map(
        local,
        mesh=mesh,
        in_specs=placed,
        out_specs=(P("dp", "weight"), P("dp", "weight"), P("weight", "dp", None, None)),
        check_vma=False,
    )
```

```python
import functools
import math

import jax
import jax.numpy as jnp
from jax import lax
from jax.experimental import pallas as pl
from jax.experimental.pallas import tpu as pltpu
from jax.sharding import PartitionSpec as P

MESH = pl.DeviceIdType.MESH
NY, NZ, NX = 4, 12, 4
F32, BF16 = jnp.float32, jnp.bfloat16


def mod(a, n):
    return lax.rem(a + n, n)


def hops(delta, side):
    long_way, short_way = NZ // 2, NZ - 1 - NZ // 2
    return long_way if (delta + side) % 2 == 0 else short_way


def greet(partners):
    barrier = pltpu.get_barrier_semaphore()
    for dp, weight in partners:
        pl.semaphore_signal(barrier, inc=1, device_id=(dp, weight), device_id_type=MESH)

    def wait():
        pl.semaphore_wait(barrier, len(partners))

    return wait


def gather_kernel(own_ref, out_ref, own_sem, y_send, y_recv, z_send, z_recv):
    dp, weight = lax.axis_index("dp"), lax.axis_index("weight")
    j, z = dp // NZ, lax.rem(dp, NZ)
    sides = (mod(z + 1, NZ), mod(z - 1, NZ))
    ready = greet(
        [(mod(j + delta, NY) * NZ + z, weight) for delta in range(1, NY)]
        + [(j * NZ + side, weight) for side in sides]
    )
    keep = pltpu.make_async_copy(own_ref, out_ref.at[dp], own_sem)
    keep.start()
    ready()

    def y_copy(delta):
        return pltpu.make_async_remote_copy(
            src_ref=own_ref,
            dst_ref=out_ref.at[dp],
            send_sem=y_send.at[delta - 1],
            recv_sem=y_recv.at[delta - 1],
            device_id=(mod(j + delta, NY) * NZ + z, weight),
            device_id_type=MESH,
        )

    def z_copy(side, delta, step):
        back = -step if side == 0 else step
        slot = mod(j - delta, NY) * NZ + mod(z + back, NZ)
        return pltpu.make_async_remote_copy(
            src_ref=own_ref if (delta == 0 and step == 0) else out_ref.at[slot],
            dst_ref=out_ref.at[slot],
            send_sem=z_send.at[side, delta, step],
            recv_sem=z_recv.at[side, delta, step],
            device_id=(j * NZ + sides[side], weight),
            device_id_type=MESH,
        )

    started = []

    def go(copy):
        copy.start()
        started.append(copy)

    def z_step(delta, step):
        for side in range(2):
            if step > hops(delta, side):
                continue
            if step > 0:
                z_copy(side, delta, step - 1).wait_recv()
            if step < hops(delta, side):
                go(z_copy(side, delta, step))

    z_step(0, 0)
    for delta in range(1, NY):
        go(y_copy(delta))
    for step in range(NZ // 2 + 1):
        z_step(0, step + 1)
        for delta in (1, 3, 2):
            if step == 0:
                y_copy(delta).wait_recv()
            z_step(delta, step)
    for copy in started:
        copy.wait_send()
    keep.wait()


def gather_blocks(own, slots):
    size = own.shape
    vmem = pl.BlockSpec(memory_space=pltpu.VMEM)
    return pl.pallas_call(
        gather_kernel,
        out_shape=jax.ShapeDtypeStruct((slots,) + size, own.dtype),
        in_specs=[vmem],
        out_specs=vmem,
        scratch_shapes=[
            pltpu.SemaphoreType.DMA,
            pltpu.SemaphoreType.DMA((NY - 1,)),
            pltpu.SemaphoreType.DMA((NY - 1,)),
            pltpu.SemaphoreType.DMA((2, NY, NZ // 2)),
            pltpu.SemaphoreType.DMA((2, NY, NZ // 2)),
        ],
        compiler_params=pltpu.CompilerParams(
            collective_id=0, has_side_effects=True, vmem_limit_bytes=4 << 20
        ),
        cost_estimate=pl.CostEstimate(flops=40_000_000_000, bytes_accessed=60_000_000, transcendentals=0),
        name="gather_blocks",
    )(own)


UNROLL = 8


def local_kernel(
    rows_ref, cols_ref, count_ref, tokens_ref, blocks_ref, cot_ref,
    act_ref, back_ref, picked_ref, spread_ref, acc_ref, grad_pre_ref, back_acc_ref,
):
    slots = blocks_ref.shape[0]
    col_blocks = grad_pre_ref.shape[0]
    row_blocks = back_acc_ref.shape[0] - 1
    count = count_ref[0]
    acc_ref[...] = jnp.zeros_like(acc_ref)

    def forward(group, carry):
        for at in range(UNROLL):
            slot = group * UNROLL + at
            live = slot < count
            col = jnp.where(live, cols_ref[0, slot], col_blocks)
            picked = tokens_ref[:, pl.ds(pl.multiple_of(rows_ref[0, slot] * 128, 128), 128)]
            picked_ref[slot] = picked * live.astype(BF16)
            acc_ref[col] += jnp.dot(picked, blocks_ref[slot], preferred_element_type=F32)
        return carry

    lax.fori_loop(0, slots // UNROLL, forward, 0)
    back_acc_ref[...] = jnp.zeros_like(back_acc_ref)
    for col in range(col_blocks):
        here = slice(col * 128, col * 128 + 128)
        preact = acc_ref[col]
        gate = jax.nn.sigmoid(preact)
        act_ref[:, here] = (preact * gate).astype(BF16)
        grad_pre_ref[col] = (
            cot_ref[:, here].astype(F32) * gate * (1.0 + preact * (1.0 - gate))
        ).astype(BF16)

    def backward(group, carry):
        for at in range(UNROLL):
            slot = group * UNROLL + at
            row = jnp.where(slot < count, rows_ref[0, slot], row_blocks)
            grad = grad_pre_ref[cols_ref[0, slot]]
            spread_ref[slot] = grad
            back_acc_ref[row] += lax.dot_general(
                grad, blocks_ref[slot], (((1,), (1,)), ((), ())), preferred_element_type=F32
            )
        return carry

    lax.fori_loop(0, slots // UNROLL, backward, 0)
    wide = back_ref.shape[2] // 128
    for row in range(row_blocks):
        at = (row % wide) * 128
        back_ref[row // wide, :, at:at + 128] = back_acc_ref[row].astype(BF16)


def local_work(rows, cols, count, tokens, blocks, cot, owners):
    tok, feat = tokens.shape
    panel = cot.shape[1]
    slots = blocks.shape[0]
    smem = pl.BlockSpec(memory_space=pltpu.SMEM)
    vmem = pl.BlockSpec(memory_space=pltpu.VMEM)
    return pl.pallas_call(
        local_kernel,
        out_shape=(
            jax.ShapeDtypeStruct((tok, panel), BF16),
            jax.ShapeDtypeStruct((owners, tok, feat // owners), BF16),
            jax.ShapeDtypeStruct((slots, tok, 128), BF16),
            jax.ShapeDtypeStruct((slots, tok, 128), BF16),
        ),
        in_specs=[smem, smem, smem, vmem, vmem, vmem],
        out_specs=(vmem, vmem, vmem, vmem),
        scratch_shapes=[
            pltpu.VMEM((panel // 128 + 1, tok, 128), F32),
            pltpu.VMEM((panel // 128, tok, 128), BF16),
            pltpu.VMEM((feat // 128 + 1, tok, 128), F32),
        ],
        compiler_params=pltpu.CompilerParams(vmem_limit_bytes=32 << 20),
        name="local_work",
    )(rows, cols, count, tokens, blocks, cot)


def reduce_kernel(
    scale, picked_ref, spread_ref, back_ref,
    in_grad_ref, block_grad_ref,
    z_buf, z_own, y_buf, y_out, c_buf, x_sum, x_buf, h_out, h_buf,
    z_send, z_recv, y_send, y_recv, c_send, c_recv, x_send, x_recv, h_send, h_recv,
):
    dp, weight = lax.axis_index("dp"), lax.axis_index("weight")
    j, z = dp // NZ, lax.rem(dp, NZ)
    x, h, core = weight // 4, lax.rem(weight // 2, 2), lax.rem(weight, 2)
    sides = (mod(z + 1, NZ), mod(z - 1, NZ))
    x_sides = (mod(x + 1, NX), mod(x - 1, NX))
    sibling = weight + 1 - 2 * core
    x_weight = [(side * 2 + h) * 2 + core for side in x_sides]
    h_weight = (x * 2 + 1 - h) * 2 + core
    ready = greet(
        [(mod(j + delta, NY) * NZ + z, weight) for delta in range(1, NY)]
        + [(j * NZ + side, weight) for side in sides]
        + [(dp, sibling)]
        + [(dp, side) for side in x_weight]
        + [(dp, h_weight)]
    )
    started = []

    def go(copy):
        copy.start()
        started.append(copy)

    def send(src, dst, send_sem, recv_sem, device):
        return pltpu.make_async_remote_copy(
            src_ref=src, dst_ref=dst, send_sem=send_sem, recv_sem=recv_sem,
            device_id=device, device_id_type=MESH,
        )

    def z_slot(side, delta, step):
        ahead = hops(delta, side) - step
        return mod(j + delta, NY) * NZ + mod(z + (ahead if side == 0 else -ahead), NZ)

    def block_grad(slot):
        return lax.dot_general(
            picked_ref[slot], spread_ref[slot], (((0,), (0,)), ((), ())),
            preferred_element_type=F32,
        )

    def z_copy(side, delta, step):
        src = z_own.at[side, delta] if step == 0 else z_buf.at[side, delta, step - 1]
        return send(
            src, z_buf.at[side, delta, step], z_send.at[side, delta, step],
            z_recv.at[side, delta, step], (j * NZ + sides[side], weight),
        )

    def z_prepare():
        for delta in range(NY):
            for side in range(2):
                z_own[side, delta] = block_grad(z_slot(side, delta, 0)).astype(BF16)

    def z_step(step):
        for delta in range(NY):
            for side in range(2):
                if step >= hops(delta, side):
                    continue
                if step > 0:
                    own = block_grad(z_slot(side, delta, step))
                    z_copy(side, delta, step - 1).wait_recv()
                    z_buf[side, delta, step - 1] = (
                        z_buf[side, delta, step - 1].astype(F32) + own
                    ).astype(BF16)
                go(z_copy(side, delta, step))

    def owner(dx, half, which):
        return (mod(x + dx, NX) * 2 + mod(h + half, 2)) * 2 + which

    def c_copy(dx, half):
        return send(
            back_ref.at[owner(dx, half, 1 - core)], c_buf.at[dx, half],
            c_send.at[dx, half], c_recv.at[dx, half], (dp, sibling),
        )

    def c_sum(dx, half):
        c_copy(dx, half).wait_recv()
        return c_buf[dx, half].astype(F32) + back_ref[owner(dx, half, core)].astype(F32)

    def x_copy(side, what):
        return send(
            x_sum.at[side, what], x_buf.at[side, what], x_send.at[side, what],
            x_recv.at[side, what], (dp, x_weight[side]),
        )

    def h_copy():
        return send(h_out, h_buf, h_send, h_recv, (dp, h_weight))

    order = [(2, 1), (2, 0), (3, 1), (1, 0), (1, 1), (3, 0), (0, 1), (0, 0)]
    z_prepare()
    ready()
    z_step(0)
    for dx, half in order:
        go(c_copy(dx, half))
    for half, side in ((1, 0), (0, 1)):
        x_sum[side, 0] = c_sum(2, half).astype(BF16)
        go(x_copy(side, 0))
    for half, side, dx in ((1, 1, 3), (0, 0, 1)):
        x_sum[side, 1] = c_sum(dx, half).astype(BF16)
        go(x_copy(side, 1))
    z_step(1)
    for half, side, dx in ((1, 0, 1), (0, 1, 3)):
        own = c_sum(dx, half)
        x_copy(side, 0).wait_recv()
        x_sum[side, 2] = (own + x_buf[side, 0].astype(F32)).astype(BF16)
        go(x_copy(side, 2))
    z_step(2)
    total = c_sum(0, 1)
    x_copy(1, 1).wait_recv()
    total += x_buf[1, 1].astype(F32)
    z_step(3)
    x_copy(0, 2).wait_recv()
    h_out[...] = (total + x_buf[0, 2].astype(F32)).astype(BF16)
    go(h_copy())
    z_step(4)
    total = c_sum(0, 0)
    x_copy(0, 1).wait_recv()
    total += x_buf[0, 1].astype(F32)
    x_copy(1, 2).wait_recv()
    total += x_buf[1, 2].astype(F32)
    z_step(5)

    def z_total(delta):
        value = block_grad(mod(j + delta, NY) * NZ + z)
        for side in range(2):
            last = hops(delta, side) - 1
            z_copy(side, delta, last).wait_recv()
            value += z_buf[side, delta, last].astype(F32)
        return value

    def y_copy(delta):
        return send(
            y_out.at[delta - 1], y_buf.at[delta - 1], y_send.at[delta - 1], y_recv.at[delta - 1],
            (mod(j + delta, NY) * NZ + z, weight),
        )

    for delta in (2, 1, 3):
        y_out[delta - 1] = z_total(delta).astype(BF16)
        go(y_copy(delta))
    grad = z_total(0)
    h_copy().wait_recv()
    in_grad_ref[...] = (total + h_buf[...].astype(F32)).astype(BF16)
    for delta in (2, 1, 3):
        y_copy(delta).wait_recv()
        grad += y_buf[delta - 1].astype(F32)
    block_grad_ref[...] = grad * scale
    for copy in started:
        copy.wait_send()


def reduce_all(picked, spread, back, scale):
    owners, tok, width = back.shape
    vmem = pl.BlockSpec(memory_space=pltpu.VMEM)
    part, block = (tok, width), (128, 128)
    dma = pltpu.SemaphoreType.DMA
    return pl.pallas_call(
        functools.partial(reduce_kernel, scale),
        out_shape=(
            jax.ShapeDtypeStruct(part, BF16),
            jax.ShapeDtypeStruct(block, F32),
        ),
        in_specs=[vmem, vmem, vmem],
        out_specs=(vmem, vmem),
        scratch_shapes=[
            pltpu.VMEM((2, NY, NZ // 2) + block, BF16),
            pltpu.VMEM((2, NY) + block, BF16),
            pltpu.VMEM((NY - 1,) + block, BF16),
            pltpu.VMEM((NY - 1,) + block, BF16),
            pltpu.VMEM((NX, 2) + part, BF16),
            pltpu.VMEM((2, 3) + part, BF16),
            pltpu.VMEM((2, 3) + part, BF16),
            pltpu.VMEM(part, BF16),
            pltpu.VMEM(part, BF16),
            dma((2, NY, NZ // 2)),
            dma((2, NY, NZ // 2)),
            dma((NY - 1,)),
            dma((NY - 1,)),
            dma((NX, 2)),
            dma((NX, 2)),
            dma((2, 3)),
            dma((2, 3)),
            dma,
            dma,
        ],
        compiler_params=pltpu.CompilerParams(
            collective_id=1, has_side_effects=True, vmem_limit_bytes=32 << 20
        ),
        name="reduce_all",
    )(picked, spread, back)


def local(tokens, block_values, block_rows, block_cols, block_counts, cotangent):
    owners = lax.axis_size("weight")
    blocks = gather_blocks(block_values[0, 0], block_rows.shape[1])
    rows, cols, count = block_rows, block_cols, block_counts
    activated, back, picked, spread = local_work(
        rows, cols, count, tokens, blocks, cotangent, owners
    )
    scale = 1.0 / math.sqrt(tokens.shape[0] * lax.axis_size("dp"))
    input_grad, block_grad = reduce_all(picked, spread, back, scale)
    return (activated, input_grad, block_grad.reshape(block_values.shape))


def solution(mesh):
    placed = (
        P("dp", None),
        P("weight", "dp", None, None),
        P("weight", None),
        P("weight", None),
        P("weight"),
        P("dp", "weight"),
    )
    return jax.shard_map(
        local,
        mesh=mesh,
        in_specs=placed,
        out_specs=(P("dp", "weight"), P("dp", "weight"), P("weight", "dp", None, None)),
        check_vma=False,
    )
```

```python
import functools
import math

import jax
import jax.numpy as jnp
from jax import lax
from jax.experimental import pallas as pl
from jax.experimental.pallas import tpu as pltpu
from jax.sharding import PartitionSpec as P

MESH = pl.DeviceIdType.MESH
NY, NZ, NX = 4, 12, 4
F32, BF16 = jnp.float32, jnp.bfloat16


GATHER_PARTS = 2
SUM_PARTS = 1


def rows_of(ref, part, parts):
    size = ref.shape[0] // parts
    return ref.at[pl.ds(part * size, size)]


def mod(a, n):
    return lax.rem(a + n, n)


def hops(delta, side):
    long_way, short_way = NZ // 2, NZ - 1 - NZ // 2
    return long_way if (delta + side) % 2 == 0 else short_way


def greet(partners):
    barrier = pltpu.get_barrier_semaphore()
    for dp, weight in partners:
        pl.semaphore_signal(barrier, inc=1, device_id=(dp, weight), device_id_type=MESH)

    def wait():
        pl.semaphore_wait(barrier, len(partners))

    return wait


def gather_kernel(own_ref, out_ref, own_sem, y_send, y_recv, z_send, z_recv):
    dp, weight = lax.axis_index("dp"), lax.axis_index("weight")
    j, z = dp // NZ, lax.rem(dp, NZ)
    sides = (mod(z + 1, NZ), mod(z - 1, NZ))
    ready = greet(
        [(mod(j + delta, NY) * NZ + z, weight) for delta in range(1, NY)]
        + [(j * NZ + side, weight) for side in sides]
    )
    keep = pltpu.make_async_copy(own_ref, out_ref.at[dp], own_sem)
    keep.start()
    ready()

    def send(src, dst, part, send_sem, recv_sem, device):
        return pltpu.make_async_remote_copy(
            src_ref=rows_of(src, part, GATHER_PARTS),
            dst_ref=rows_of(dst, part, GATHER_PARTS),
            send_sem=send_sem,
            recv_sem=recv_sem,
            device_id=(device, weight),
            device_id_type=MESH,
        )

    def y_copy(delta, part):
        at = (delta - 1, part)
        return send(
            own_ref, out_ref.at[dp], part, y_send.at[at], y_recv.at[at],
            mod(j + delta, NY) * NZ + z,
        )

    def z_copy(side, delta, step, part):
        back = -step if side == 0 else step
        slot = mod(j - delta, NY) * NZ + mod(z + back, NZ)
        src = own_ref if (delta == 0 and step == 0) else out_ref.at[slot]
        at = (side, delta, step, part)
        return send(
            src, out_ref.at[slot], part, z_send.at[at], z_recv.at[at], j * NZ + sides[side]
        )

    started = []

    def go(copy):
        copy.start()
        started.append(copy)

    def z_step(delta, step, part):
        for side in range(2):
            if step > hops(delta, side):
                continue
            if step > 0:
                z_copy(side, delta, step - 1, part).wait_recv()
            if step < hops(delta, side):
                go(z_copy(side, delta, step, part))

    for part in range(GATHER_PARTS):
        z_step(0, 0, part)
    for part in range(GATHER_PARTS):
        for delta in range(1, NY):
            go(y_copy(delta, part))
    for step in range(NZ // 2 + 1):
        for part in range(GATHER_PARTS):
            z_step(0, step + 1, part)
        for part in range(GATHER_PARTS):
            for delta in (1, 3, 2):
                if step == 0:
                    y_copy(delta, part).wait_recv()
                z_step(delta, step, part)
    for copy in started:
        copy.wait_send()
    keep.wait()


def gather_blocks(own, slots):
    size = own.shape
    vmem = pl.BlockSpec(memory_space=pltpu.VMEM)
    return pl.pallas_call(
        gather_kernel,
        out_shape=jax.ShapeDtypeStruct((slots,) + size, own.dtype),
        in_specs=[vmem],
        out_specs=vmem,
        scratch_shapes=[
            pltpu.SemaphoreType.DMA,
            pltpu.SemaphoreType.DMA((NY - 1, GATHER_PARTS)),
            pltpu.SemaphoreType.DMA((NY - 1, GATHER_PARTS)),
            pltpu.SemaphoreType.DMA((2, NY, NZ // 2, GATHER_PARTS)),
            pltpu.SemaphoreType.DMA((2, NY, NZ // 2, GATHER_PARTS)),
        ],
        compiler_params=pltpu.CompilerParams(
            collective_id=0, has_side_effects=True, vmem_limit_bytes=4 << 20
        ),
        cost_estimate=pl.CostEstimate(flops=40_000_000_000, bytes_accessed=60_000_000, transcendentals=0),
        name="gather_blocks",
    )(own)


UNROLL = 24


def local_kernel(
    rows_ref, cols_ref, count_ref, tokens_ref, blocks_ref, cot_ref,
    act_ref, picked_ref, spread_ref, before_ref, last_ref, acc_ref, grad_pre_ref,
):
    slots = blocks_ref.shape[0]
    col_blocks = grad_pre_ref.shape[0]
    count = count_ref[0]
    for row in range(last_ref.shape[0]):
        last_ref[row] = slots
    for slot in range(slots):
        row = rows_ref[0, slot]
        known = last_ref[row]
        before_ref[slot] = known
        last_ref[row] = jnp.where(slot < count, slot, known)
    acc_ref[...] = jnp.zeros_like(acc_ref)

    def forward(group, carry):
        for at in range(UNROLL):
            slot = group * UNROLL + at
            live = slot < count
            col = jnp.where(live, cols_ref[0, slot], col_blocks)
            picked = tokens_ref[:, pl.ds(pl.multiple_of(rows_ref[0, slot] * 128, 128), 128)]
            picked_ref[slot] = picked * live.astype(BF16)
            acc_ref[col] += jnp.dot(picked, blocks_ref[slot], preferred_element_type=F32)
        return carry

    lax.fori_loop(0, slots // UNROLL, forward, 0)
    for col in range(col_blocks):
        here = slice(col * 128, col * 128 + 128)
        preact = acc_ref[col]
        gate = jax.nn.sigmoid(preact)
        act_ref[:, here] = (preact * gate).astype(BF16)
        grad_pre_ref[col] = (
            cot_ref[:, here].astype(F32) * gate * (1.0 + preact * (1.0 - gate))
        ).astype(BF16)

    for slot in range(slots):
        spread_ref[slot] = grad_pre_ref[cols_ref[0, slot]]


def local_work(rows, cols, count, tokens, blocks, cot):
    tok, feat = tokens.shape
    panel = cot.shape[1]
    slots = blocks.shape[0]
    smem = pl.BlockSpec(memory_space=pltpu.SMEM)
    vmem = pl.BlockSpec(memory_space=pltpu.VMEM)
    return pl.pallas_call(
        local_kernel,
        out_shape=(
            jax.ShapeDtypeStruct((tok, panel), BF16),
            jax.ShapeDtypeStruct((slots, tok, 128), BF16),
            jax.ShapeDtypeStruct((slots, tok, 128), BF16),
            jax.ShapeDtypeStruct((slots,), jnp.int32),
            jax.ShapeDtypeStruct((feat // 128,), jnp.int32),
        ),
        in_specs=[smem, smem, smem, vmem, vmem, vmem],
        out_specs=(vmem, vmem, vmem, smem, smem),
        scratch_shapes=[
            pltpu.VMEM((panel // 128 + 1, tok, 128), F32),
            pltpu.VMEM((panel // 128, tok, 128), BF16),
        ],
        compiler_params=pltpu.CompilerParams(vmem_limit_bytes=32 << 20),
        name="local_work",
    )(rows, cols, count, tokens, blocks, cot)


def reduce_kernel(
    scale, before_ref, last_ref, picked_ref, spread_ref, blocks_ref, in_grad_ref, block_grad_ref,
    terms, back_ref, z_buf, z_own, z_first, y_buf, y_out, c_buf, x_sum, x_buf, h_out, h_buf,
    z_send, z_recv, y_send, y_recv, c_send, c_recv, x_send, x_recv, h_send, h_recv,
):
    dp, weight = lax.axis_index("dp"), lax.axis_index("weight")
    j, z = dp // NZ, lax.rem(dp, NZ)
    x, h, core = weight // 4, lax.rem(weight // 2, 2), lax.rem(weight, 2)
    sides = (mod(z + 1, NZ), mod(z - 1, NZ))
    x_sides = (mod(x + 1, NX), mod(x - 1, NX))
    sibling = weight + 1 - 2 * core
    x_weight = [(side * 2 + h) * 2 + core for side in x_sides]
    h_weight = (x * 2 + 1 - h) * 2 + core
    ready = greet(
        [(mod(j + delta, NY) * NZ + z, weight) for delta in range(1, NY)]
        + [(j * NZ + side, weight) for side in sides]
        + [(dp, sibling)]
        + [(dp, side) for side in x_weight]
        + [(dp, h_weight)]
    )
    started = []

    def go(copy):
        copy.start()
        started.append(copy)

    def send(src, dst, send_sem, recv_sem, device):
        return pltpu.make_async_remote_copy(
            src_ref=src, dst_ref=dst, send_sem=send_sem, recv_sem=recv_sem,
            device_id=device, device_id_type=MESH,
        )

    def z_slot(side, delta, step):
        ahead = hops(delta, side) - step
        return mod(j + delta, NY) * NZ + mod(z + (ahead if side == 0 else -ahead), NZ)

    def block_grad(slot):
        return lax.dot_general(
            picked_ref[slot], spread_ref[slot], (((0,), (0,)), ((), ())),
            preferred_element_type=F32,
        )

    def z_copy(side, delta, step, part):
        src = z_first.at[side, delta] if step == 0 else z_buf.at[side, delta, step - 1]
        at = (side, delta, step, part)
        return send(
            rows_of(src, part, SUM_PARTS), rows_of(z_buf.at[side, delta, step], part, SUM_PARTS),
            z_send.at[at], z_recv.at[at], (j * NZ + sides[side], weight),
        )

    def streams(step):
        return [(d, side) for d in range(NY) for side in range(2) if step < hops(d, side)]

    def z_prepare(step):
        for delta, side in streams(step):
            own = block_grad(z_slot(side, delta, step))
            if step == 0:
                z_first[side, delta] = own.astype(BF16)
            else:
                z_own[side, delta] = own

    def z_step(step):
        size = 128 // SUM_PARTS
        for part in range(SUM_PARTS):
            here = slice(part * size, part * size + size)
            for delta, side in streams(step):
                if step > 0:
                    z_copy(side, delta, step - 1, part).wait_recv()
                    z_buf[side, delta, step - 1, here] = (
                        z_buf[side, delta, step - 1, here].astype(F32) + z_own[side, delta, here]
                    ).astype(BF16)
                go(z_copy(side, delta, step, part))

    def back_terms():
        slots = blocks_ref.shape[0]
        terms[slots] = jnp.zeros_like(terms[slots])
        for slot in range(slots):
            terms[slot] = terms[before_ref[slot]] + lax.dot_general(
                spread_ref[slot], blocks_ref[slot], (((1,), (1,)), ((), ())),
                preferred_element_type=F32,
            )
        wide = back_ref.shape[2] // 128
        for row in range(last_ref.shape[0]):
            at = (row % wide) * 128
            back_ref[row // wide, :, at:at + 128] = terms[last_ref[row]].astype(BF16)

    def owner(dx, half, which):
        return (mod(x + dx, NX) * 2 + mod(h + half, 2)) * 2 + which

    def c_copy(dx, half):
        return send(
            back_ref.at[owner(dx, half, 1 - core)], c_buf.at[dx, half],
            c_send.at[dx, half], c_recv.at[dx, half], (dp, sibling),
        )

    def c_sum(dx, half):
        c_copy(dx, half).wait_recv()
        return c_buf[dx, half].astype(F32) + back_ref[owner(dx, half, core)].astype(F32)

    def x_copy(side, what, part=0, parts=1):
        at = (side, what, part)
        return send(
            rows_of(x_sum.at[side, what], part, parts), rows_of(x_buf.at[side, what], part, parts),
            x_send.at[at], x_recv.at[at], (dp, x_weight[side]),
        )

    def h_copy(part):
        return send(
            rows_of(h_out, part, 2), rows_of(h_buf, part, 2), h_send.at[part], h_recv.at[part],
            (dp, h_weight),
        )

    half_rows = h_out.shape[0] // 2
    halves = [(part, slice(part * half_rows, part * half_rows + half_rows)) for part in range(2)]

    z_prepare(0)
    ready()
    z_step(0)
    z_prepare(1)
    back_terms()
    for dx, half in [(2, 1), (2, 0), (1, 1), (3, 0), (1, 0), (3, 1), (0, 1), (0, 0)]:
        go(c_copy(dx, half))
    z_step(1)
    z_prepare(2)
    x_sum[0, 0] = c_sum(2, 1).astype(BF16)
    for part in range(2):
        go(x_copy(0, 0, part, 2))
    x_sum[1, 0] = c_sum(2, 0).astype(BF16)
    go(x_copy(1, 0))
    z_step(2)
    z_prepare(3)
    own_right, own_left = c_sum(1, 1), c_sum(3, 0)
    z_step(3)
    z_prepare(4)
    for part, here in halves:
        x_copy(0, 0, part, 2).wait_recv()
        x_sum[0, 2, here] = (own_right[here] + x_buf[0, 0, here].astype(F32)).astype(BF16)
        go(x_copy(0, 2, part, 2))
    x_sum[1, 1] = c_sum(3, 1).astype(BF16)
    go(x_copy(1, 1))
    x_sum[0, 1] = c_sum(1, 0).astype(BF16)
    go(x_copy(0, 1))
    z_step(4)
    z_prepare(5)
    x_copy(1, 0).wait_recv()
    x_sum[1, 2] = (own_left + x_buf[1, 0].astype(F32)).astype(BF16)
    go(x_copy(1, 2))
    total = c_sum(0, 1)
    z_step(5)
    x_copy(1, 1).wait_recv()
    total += x_buf[1, 1].astype(F32)
    for part, here in halves:
        x_copy(0, 2, part, 2).wait_recv()
        h_out[here] = (total[here] + x_buf[0, 2, here].astype(F32)).astype(BF16)
        go(h_copy(part))
    kept = [block_grad(mod(j + delta, NY) * NZ + z) for delta in range(NY)]

    def z_total(delta):
        value = kept[delta]
        for side in range(2):
            last = hops(delta, side) - 1
            for part in range(SUM_PARTS):
                z_copy(side, delta, last, part).wait_recv()
            value += z_buf[side, delta, last].astype(F32)
        return value

    def y_copy(delta):
        return send(
            y_out.at[delta - 1], y_buf.at[delta - 1], y_send.at[delta - 1], y_recv.at[delta - 1],
            (mod(j + delta, NY) * NZ + z, weight),
        )

    for delta in (2, 1, 3):
        y_out[delta - 1] = z_total(delta).astype(BF16)
        go(y_copy(delta))
    grad = z_total(0)
    total = c_sum(0, 0)
    x_copy(0, 1).wait_recv()
    total += x_buf[0, 1].astype(F32)
    x_copy(1, 2).wait_recv()
    total += x_buf[1, 2].astype(F32)
    for delta in (1, 3, 2):
        y_copy(delta).wait_recv()
        grad += y_buf[delta - 1].astype(F32)
    block_grad_ref[...] = grad * scale
    for part, here in halves:
        h_copy(part).wait_recv()
        in_grad_ref[here] = (total[here] + h_buf[here].astype(F32)).astype(BF16)
    for copy in started:
        copy.wait_send()


def reduce_all(before, last, picked, spread, blocks, owners, scale):
    slots, tok = picked.shape[:2]
    vmem, smem = pl.BlockSpec(memory_space=pltpu.VMEM), pl.BlockSpec(memory_space=pltpu.SMEM)
    part, block = (tok, last.shape[0] * 128 // owners), (128, 128)
    dma = pltpu.SemaphoreType.DMA
    return pl.pallas_call(
        functools.partial(reduce_kernel, scale),
        out_shape=(
            jax.ShapeDtypeStruct(part, BF16),
            jax.ShapeDtypeStruct(block, F32),
        ),
        in_specs=[smem, smem, vmem, vmem, vmem],
        out_specs=(vmem, vmem),
        scratch_shapes=[
            pltpu.VMEM((slots + 1, tok, 128), F32),
            pltpu.VMEM((owners,) + part, BF16),
            pltpu.VMEM((2, NY, NZ // 2) + block, BF16),
            pltpu.VMEM((2, NY) + block, F32),
            pltpu.VMEM((2, NY) + block, BF16),
            pltpu.VMEM((NY - 1,) + block, BF16),
            pltpu.VMEM((NY - 1,) + block, BF16),
            pltpu.VMEM((NX, 2) + part, BF16),
            pltpu.VMEM((2, 3) + part, BF16),
            pltpu.VMEM((2, 3) + part, BF16),
            pltpu.VMEM(part, BF16),
            pltpu.VMEM(part, BF16),
            dma((2, NY, NZ // 2, SUM_PARTS)),
            dma((2, NY, NZ // 2, SUM_PARTS)),
            dma((NY - 1,)),
            dma((NY - 1,)),
            dma((NX, 2)),
            dma((NX, 2)),
            dma((2, 3, 2)),
            dma((2, 3, 2)),
            dma((2,)),
            dma((2,)),
        ],
        compiler_params=pltpu.CompilerParams(
            collective_id=1, has_side_effects=True, vmem_limit_bytes=32 << 20
        ),
        name="reduce_all",
    )(before, last, picked, spread, blocks)


def local(tokens, block_values, block_rows, block_cols, block_counts, cotangent):
    owners = lax.axis_size("weight")
    blocks = gather_blocks(block_values[0, 0], block_rows.shape[1])
    rows, cols, count = block_rows, block_cols, block_counts
    activated, picked, spread, before, last = local_work(
        rows, cols, count, tokens, blocks, cotangent
    )
    scale = 1.0 / math.sqrt(tokens.shape[0] * lax.axis_size("dp"))
    input_grad, block_grad = reduce_all(before, last, picked, spread, blocks, owners, scale)
    return (activated, input_grad, block_grad.reshape(block_values.shape))


def solution(mesh):
    placed = (
        P("dp", None),
        P("weight", "dp", None, None),
        P("weight", None),
        P("weight", None),
        P("weight"),
        P("dp", "weight"),
    )
    return jax.shard_map(
        local,
        mesh=mesh,
        in_specs=placed,
        out_specs=(P("dp", "weight"), P("dp", "weight"), P("weight", "dp", None, None)),
        check_vma=False,
    )
```

```python
import functools
import math

import jax
import jax.numpy as jnp
from jax import lax
from jax.experimental import pallas as pl
from jax.experimental.pallas import tpu as pltpu
from jax.sharding import PartitionSpec as P

MESH = pl.DeviceIdType.MESH
NY, NZ, NX = 4, 12, 4
F32, BF16 = jnp.float32, jnp.bfloat16


Y_ROWS = 96


def stripe(ref, delta):
    return ref if delta == 0 else ref.at[pl.ds(0, Y_ROWS)]


def rest(ref):
    return ref.at[pl.ds(Y_ROWS, ref.shape[0] - Y_ROWS)]


def rows_of(ref, part, parts):
    size = ref.shape[0] // parts
    return ref.at[pl.ds(part * size, size)]


def mod(a, n):
    return lax.rem(a + n, n)


def hops(delta, side):
    long_way, short_way = NZ // 2, NZ - 1 - NZ // 2
    return long_way if (delta + side) % 2 == 0 else short_way


LONG = NZ // 2


def is_long(delta, side):
    return hops(delta, side) == LONG


def greet(partners):
    barrier = pltpu.get_barrier_semaphore()
    for dp, weight in partners:
        pl.semaphore_signal(barrier, inc=1, device_id=(dp, weight), device_id_type=MESH)

    def wait():
        pl.semaphore_wait(barrier, len(partners))

    return wait


def gather_kernel(own_ref, out_ref, own_sem, y_send, y_recv, z_send, z_recv, r_send, r_recv):
    dp, weight = lax.axis_index("dp"), lax.axis_index("weight")
    j, z = dp // NZ, lax.rem(dp, NZ)
    sides = (mod(z + 1, NZ), mod(z - 1, NZ))
    far = (mod(z + 2, NZ), mod(z - 2, NZ))
    ready = greet(
        [(mod(j + delta, NY) * NZ + z, weight) for delta in range(1, NY)]
        + [(j * NZ + side, weight) for side in sides + far]
    )
    keep = pltpu.make_async_copy(own_ref, out_ref.at[dp], own_sem)
    keep.start()
    ready()

    def send(src, dst, send_sem, recv_sem, device):
        return pltpu.make_async_remote_copy(
            src_ref=src, dst_ref=dst, send_sem=send_sem, recv_sem=recv_sem,
            device_id=(device, weight), device_id_type=MESH,
        )

    def y_copy(delta):
        return send(
            own_ref, out_ref.at[dp], y_send.at[delta - 1], y_recv.at[delta - 1],
            mod(j + delta, NY) * NZ + z,
        )

    def z_copy(side, delta, step):
        held = min(step, LONG - 2)
        back = -held if side == 0 else held
        slot = mod(j - delta, NY) * NZ + mod(z + back, NZ)
        src = own_ref if (delta == 0 and step == 0) else out_ref.at[slot]
        at = (side, delta, step)
        return send(
            stripe(src, delta), stripe(out_ref.at[slot], delta), z_send.at[at], z_recv.at[at],
            j * NZ + (far if step == LONG - 1 else sides)[side],
        )

    def rest_copy(delta, side, step):
        back = -step - 1 if side == 0 else step + 1
        slot = j * NZ + mod(z + back, NZ)
        at = (delta - 1, side, step)
        return send(
            rest(out_ref.at[slot]), rest(out_ref.at[slot]), r_send.at[at], r_recv.at[at],
            mod(j + delta, NY) * NZ + z,
        )

    started = []

    def go(copy):
        copy.start()
        started.append(copy)

    def z_step(delta, step):
        for side in range(2):
            if step > hops(delta, side):
                continue
            if step > 0:
                z_copy(side, delta, step - 1).wait_recv()
            if step < min(hops(delta, side), LONG - 1):
                go(z_copy(side, delta, step))
            if step == LONG - 2 and is_long(delta, side):
                go(z_copy(side, delta, LONG - 1))
        for side in range(2):
            if delta == 0 and 0 < step <= hops(0, side):
                for other in range(1, NY):
                    go(rest_copy(other, side, step - 1))

    z_step(0, 0)
    for delta in range(1, NY):
        go(y_copy(delta))
    for step in range(NZ // 2 + 1):
        z_step(0, step + 1)
        for delta in (1, 3, 2):
            if step == 0:
                y_copy(delta).wait_recv()
            z_step(delta, step)
    for side in range(2):
        for step in range(hops(0, side)):
            for delta in range(1, NY):
                rest_copy(delta, side, step).wait_recv()
    for copy in started:
        copy.wait_send()
    keep.wait()


def gather_blocks(own, slots):
    size = own.shape
    vmem = pl.BlockSpec(memory_space=pltpu.VMEM)
    return pl.pallas_call(
        gather_kernel,
        out_shape=jax.ShapeDtypeStruct((slots,) + size, own.dtype),
        in_specs=[vmem],
        out_specs=vmem,
        scratch_shapes=[
            pltpu.SemaphoreType.DMA,
            pltpu.SemaphoreType.DMA((NY - 1,)),
            pltpu.SemaphoreType.DMA((NY - 1,)),
            pltpu.SemaphoreType.DMA((2, NY, NZ // 2)),
            pltpu.SemaphoreType.DMA((2, NY, NZ // 2)),
            pltpu.SemaphoreType.DMA((NY - 1, 2, NZ // 2)),
            pltpu.SemaphoreType.DMA((NY - 1, 2, NZ // 2)),
        ],
        compiler_params=pltpu.CompilerParams(
            collective_id=0, has_side_effects=True, vmem_limit_bytes=4 << 20
        ),
        cost_estimate=pl.CostEstimate(flops=40_000_000_000, bytes_accessed=60_000_000, transcendentals=0),
        name="gather_blocks",
    )(own)


UNROLL = 24


def local_kernel(
    rows_ref, cols_ref, count_ref, tokens_ref, blocks_ref, cot_ref,
    act_ref, picked_ref, spread_ref, before_ref, last_ref, acc_ref, grad_pre_ref,
):
    slots = blocks_ref.shape[0]
    col_blocks = grad_pre_ref.shape[0]
    count = count_ref[0]
    for row in range(last_ref.shape[0]):
        last_ref[row] = slots
    for slot in range(slots):
        row = rows_ref[0, slot]
        known = last_ref[row]
        before_ref[slot] = known
        last_ref[row] = jnp.where(slot < count, slot, known)
    acc_ref[...] = jnp.zeros_like(acc_ref)

    def forward(group, carry):
        for at in range(UNROLL):
            slot = group * UNROLL + at
            live = slot < count
            col = jnp.where(live, cols_ref[0, slot], col_blocks)
            picked = tokens_ref[:, pl.ds(pl.multiple_of(rows_ref[0, slot] * 128, 128), 128)]
            picked_ref[slot] = picked * live.astype(BF16)
            acc_ref[col] += jnp.dot(picked, blocks_ref[slot], preferred_element_type=F32)
        return carry

    lax.fori_loop(0, slots // UNROLL, forward, 0)
    for col in range(col_blocks):
        here = slice(col * 128, col * 128 + 128)
        preact = acc_ref[col]
        gate = jax.nn.sigmoid(preact)
        act_ref[:, here] = (preact * gate).astype(BF16)
        grad_pre_ref[col] = (
            cot_ref[:, here].astype(F32) * gate * (1.0 + preact * (1.0 - gate))
        ).astype(BF16)

    for slot in range(slots):
        spread_ref[slot] = grad_pre_ref[cols_ref[0, slot]]


def local_work(rows, cols, count, tokens, blocks, cot):
    tok, feat = tokens.shape
    panel = cot.shape[1]
    slots = blocks.shape[0]
    smem = pl.BlockSpec(memory_space=pltpu.SMEM)
    vmem = pl.BlockSpec(memory_space=pltpu.VMEM)
    return pl.pallas_call(
        local_kernel,
        out_shape=(
            jax.ShapeDtypeStruct((tok, panel), BF16),
            jax.ShapeDtypeStruct((slots, tok, 128), BF16),
            jax.ShapeDtypeStruct((slots, tok, 128), BF16),
            jax.ShapeDtypeStruct((slots,), jnp.int32),
            jax.ShapeDtypeStruct((feat // 128,), jnp.int32),
        ),
        in_specs=[smem, smem, smem, vmem, vmem, vmem],
        out_specs=(vmem, vmem, vmem, smem, smem),
        scratch_shapes=[
            pltpu.VMEM((panel // 128 + 1, tok, 128), F32),
            pltpu.VMEM((panel // 128, tok, 128), BF16),
        ],
        compiler_params=pltpu.CompilerParams(vmem_limit_bytes=32 << 20),
        name="local_work",
    )(rows, cols, count, tokens, blocks, cot)


def reduce_kernel(
    scale, before_ref, last_ref, picked_ref, spread_ref, blocks_ref, in_grad_ref, block_grad_ref,
    terms, back_ref, z_buf, z_own, z_first, r_buf, r_out, y_buf, y_out, c_buf, x_sum, x_buf, h_out, h_buf,
    z_send, z_recv, r_send, r_recv, y_send, y_recv, c_send, c_recv, x_send, x_recv,
    h_send, h_recv,
):
    dp, weight = lax.axis_index("dp"), lax.axis_index("weight")
    j, z = dp // NZ, lax.rem(dp, NZ)
    x, h, core = weight // 4, lax.rem(weight // 2, 2), lax.rem(weight, 2)
    sides = (mod(z + 1, NZ), mod(z - 1, NZ))
    far = (mod(z + 2, NZ), mod(z - 2, NZ))
    x_sides = (mod(x + 1, NX), mod(x - 1, NX))
    sibling = weight + 1 - 2 * core
    x_weight = [(side * 2 + h) * 2 + core for side in x_sides]
    h_weight = (x * 2 + 1 - h) * 2 + core
    ready = greet(
        [(mod(j + delta, NY) * NZ + z, weight) for delta in range(1, NY)]
        + [(j * NZ + side, weight) for side in sides + far]
        + [(dp, sibling)]
        + [(dp, side) for side in x_weight]
        + [(dp, h_weight)]
    )
    started = []

    def go(copy):
        copy.start()
        started.append(copy)

    def send(src, dst, send_sem, recv_sem, device):
        return pltpu.make_async_remote_copy(
            src_ref=src, dst_ref=dst, send_sem=send_sem, recv_sem=recv_sem,
            device_id=device, device_id_type=MESH,
        )

    def offset(side, delta, step):
        ahead = hops(delta, side) - step
        return ahead if side == 0 else NZ - ahead

    def block_grad(delta, off):
        slot = mod(j + delta, NY) * NZ + mod(z + off, NZ)
        z_own[delta, off] = lax.dot_general(
            picked_ref[slot], spread_ref[slot], (((0,), (0,)), ((), ())),
            preferred_element_type=F32,
        )
        if delta > 0 and off > 0:
            r_out[delta - 1, off] = z_own[delta, off, Y_ROWS:].astype(BF16)

    def rest_copy(delta, off):
        at = (delta - 1, off)
        return send(
            r_out.at[at], r_buf.at[at], r_send.at[at], r_recv.at[at],
            (mod(j + delta, NY) * NZ + z, weight),
        )

    def z_copy(side, delta, step):
        if step == 0 or (step == 1 and is_long(delta, side)):
            src = z_first.at[side, delta, step]
        else:
            src = z_buf.at[side, delta, step - 1]
        at = (side, delta, step)
        target = far if step == 0 and is_long(delta, side) else sides
        return send(
            stripe(src, delta), stripe(z_buf.at[at], delta), z_send.at[at], z_recv.at[at],
            (j * NZ + target[side], weight),
        )

    def z_add(side, delta, step):
        off = offset(side, delta, step)
        if delta == 0:
            for other in range(1, NY):
                rest_copy(other, off).wait_recv()
                z_own[0, off, Y_ROWS:] += r_buf[other - 1, off].astype(F32)
        many = 128 if delta == 0 else Y_ROWS
        own = z_own[delta, off, :many]
        if step == 0 or (step == 1 and is_long(delta, side)):
            z_first[side, delta, step, :many] = own.astype(BF16)
        else:
            if step == 2 and is_long(delta, side):
                z_copy(side, delta, 0).wait_recv()
                own += z_buf[side, delta, 0, :many].astype(F32)
            z_copy(side, delta, step - 1).wait_recv()
            z_buf[side, delta, step - 1, :many] = (
                z_buf[side, delta, step - 1, :many].astype(F32) + own
            ).astype(BF16)
        go(z_copy(side, delta, step))

    def z_step(turn, deltas):
        for delta in deltas:
            for side in range(2):
                if turn == 0:
                    z_add(side, delta, 0)
                if is_long(delta, side):
                    z_add(side, delta, turn + 1)
                elif turn > 0:
                    z_add(side, delta, turn)

    def back_terms():
        slots = blocks_ref.shape[0]
        terms[slots] = jnp.zeros_like(terms[slots])
        for slot in range(slots):
            terms[slot] = terms[before_ref[slot]] + lax.dot_general(
                spread_ref[slot], blocks_ref[slot], (((1,), (1,)), ((), ())),
                preferred_element_type=F32,
            )
        wide = back_ref.shape[2] // 128
        for row in range(last_ref.shape[0]):
            at = (row % wide) * 128
            back_ref[row // wide, :, at:at + 128] = terms[last_ref[row]].astype(BF16)

    def owner(dx, half, which):
        return (mod(x + dx, NX) * 2 + mod(h + half, 2)) * 2 + which

    def c_copy(dx, half):
        return send(
            back_ref.at[owner(dx, half, 1 - core)], c_buf.at[dx, half],
            c_send.at[dx, half], c_recv.at[dx, half], (dp, sibling),
        )

    def c_sum(dx, half):
        c_copy(dx, half).wait_recv()
        return c_buf[dx, half].astype(F32) + back_ref[owner(dx, half, core)].astype(F32)

    def x_copy(side, what, part=0, parts=1):
        at = (side, what, part)
        return send(
            rows_of(x_sum.at[side, what], part, parts), rows_of(x_buf.at[side, what], part, parts),
            x_send.at[at], x_recv.at[at], (dp, x_weight[side]),
        )

    def h_copy(part):
        return send(
            rows_of(h_out, part, 2), rows_of(h_buf, part, 2), h_send.at[part], h_recv.at[part],
            (dp, h_weight),
        )

    half_rows = h_out.shape[0] // 2
    halves = [(part, slice(part * half_rows, part * half_rows + half_rows)) for part in range(2)]

    others, own = (2, 1, 3), (0,)
    middle = NZ // 2
    offs = sorted(range(NZ), key=lambda off: (abs(off - middle), off > middle))
    first = offs[:3]
    for off in first:
        for delta in range(NY):
            block_grad(delta, off)
    ready()
    for off in first:
        for delta in range(1, NY):
            go(rest_copy(delta, off))
    z_step(0, others)
    for off in offs[3:]:
        for delta in range(NY):
            block_grad(delta, off)
        if off > 0:
            for delta in range(1, NY):
                go(rest_copy(delta, off))
    back_terms()
    for dx, half in [(2, 1), (2, 0), (1, 1), (3, 0), (1, 0), (3, 1), (0, 1), (0, 0)]:
        go(c_copy(dx, half))
    z_step(1, others)
    z_step(0, own)
    x_sum[0, 0] = c_sum(2, 1).astype(BF16)
    for part in range(2):
        go(x_copy(0, 0, part, 2))
    x_sum[1, 0] = c_sum(2, 0).astype(BF16)
    go(x_copy(1, 0))
    z_step(2, others)
    z_step(1, own)
    own_right, own_left = c_sum(1, 1), c_sum(3, 0)
    for part, here in halves:
        x_copy(0, 0, part, 2).wait_recv()
        x_sum[0, 2, here] = (own_right[here] + x_buf[0, 0, here].astype(F32)).astype(BF16)
        go(x_copy(0, 2, part, 2))
    z_step(3, others)
    z_step(2, own)
    x_sum[1, 1] = c_sum(3, 1).astype(BF16)
    go(x_copy(1, 1))
    x_sum[0, 1] = c_sum(1, 0).astype(BF16)
    go(x_copy(0, 1))
    x_copy(1, 0).wait_recv()
    x_sum[1, 2] = (own_left + x_buf[1, 0].astype(F32)).astype(BF16)
    go(x_copy(1, 2))
    total = c_sum(0, 1)
    z_step(4, others)
    z_step(3, own)
    x_copy(1, 1).wait_recv()
    total += x_buf[1, 1].astype(F32)
    for part, here in halves:
        x_copy(0, 2, part, 2).wait_recv()
        h_out[here] = (total[here] + x_buf[0, 2, here].astype(F32)).astype(BF16)
        go(h_copy(part))

    def z_total(delta):
        many = 128 if delta == 0 else Y_ROWS
        for side in range(2):
            last = hops(delta, side) - 1
            z_copy(side, delta, last).wait_recv()
            z_own[delta, 0, :many] += z_buf[side, delta, last, :many].astype(F32)
        return z_own[delta, 0]

    def y_copy(delta):
        return send(
            y_out.at[delta - 1], y_buf.at[delta - 1], y_send.at[delta - 1], y_recv.at[delta - 1],
            (mod(j + delta, NY) * NZ + z, weight),
        )

    for delta in others:
        y_out[delta - 1] = z_total(delta).astype(BF16)
        go(y_copy(delta))
    z_step(4, own)
    grad = z_total(0)
    total = c_sum(0, 0)
    x_copy(0, 1).wait_recv()
    total += x_buf[0, 1].astype(F32)
    x_copy(1, 2).wait_recv()
    total += x_buf[1, 2].astype(F32)
    for delta in (1, 3, 2):
        y_copy(delta).wait_recv()
        grad += y_buf[delta - 1].astype(F32)
    block_grad_ref[...] = grad * scale
    for part, here in halves:
        h_copy(part).wait_recv()
        in_grad_ref[here] = (total[here] + h_buf[here].astype(F32)).astype(BF16)
    for copy in started:
        copy.wait_send()


def reduce_all(before, last, picked, spread, blocks, owners, scale):
    slots, tok = picked.shape[:2]
    vmem, smem = pl.BlockSpec(memory_space=pltpu.VMEM), pl.BlockSpec(memory_space=pltpu.SMEM)
    part, block = (tok, last.shape[0] * 128 // owners), (128, 128)
    dma = pltpu.SemaphoreType.DMA
    return pl.pallas_call(
        functools.partial(reduce_kernel, scale),
        out_shape=(
            jax.ShapeDtypeStruct(part, BF16),
            jax.ShapeDtypeStruct(block, F32),
        ),
        in_specs=[smem, smem, vmem, vmem, vmem],
        out_specs=(vmem, vmem),
        scratch_shapes=[
            pltpu.VMEM((slots + 1, tok, 128), F32),
            pltpu.VMEM((owners,) + part, BF16),
            pltpu.VMEM((2, NY, NZ // 2) + block, BF16),
            pltpu.VMEM((NY, NZ) + block, F32),
            pltpu.VMEM((2, NY, 2) + block, BF16),
            pltpu.VMEM((NY - 1, NZ, 128 - Y_ROWS, 128), BF16),
            pltpu.VMEM((NY - 1, NZ, 128 - Y_ROWS, 128), BF16),
            pltpu.VMEM((NY - 1,) + block, BF16),
            pltpu.VMEM((NY - 1,) + block, BF16),
            pltpu.VMEM((NX, 2) + part, BF16),
            pltpu.VMEM((2, 3) + part, BF16),
            pltpu.VMEM((2, 3) + part, BF16),
            pltpu.VMEM(part, BF16),
            pltpu.VMEM(part, BF16),
            dma((2, NY, NZ // 2)),
            dma((2, NY, NZ // 2)),
            dma((NY - 1, NZ)),
            dma((NY - 1, NZ)),
            dma((NY - 1,)),
            dma((NY - 1,)),
            dma((NX, 2)),
            dma((NX, 2)),
            dma((2, 3, 2)),
            dma((2, 3, 2)),
            dma((2,)),
            dma((2,)),
        ],
        compiler_params=pltpu.CompilerParams(
            collective_id=1, has_side_effects=True, vmem_limit_bytes=32 << 20
        ),
        name="reduce_all",
    )(before, last, picked, spread, blocks)


def local(tokens, block_values, block_rows, block_cols, block_counts, cotangent):
    owners = lax.axis_size("weight")
    blocks = gather_blocks(block_values[0, 0], block_rows.shape[1])
    rows, cols, count = block_rows, block_cols, block_counts
    activated, picked, spread, before, last = local_work(
        rows, cols, count, tokens, blocks, cotangent
    )
    scale = 1.0 / math.sqrt(tokens.shape[0] * lax.axis_size("dp"))
    input_grad, block_grad = reduce_all(before, last, picked, spread, blocks, owners, scale)
    return (activated, input_grad, block_grad.reshape(block_values.shape))


def solution(mesh):
    placed = (
        P("dp", None),
        P("weight", "dp", None, None),
        P("weight", None),
        P("weight", None),
        P("weight"),
        P("dp", "weight"),
    )
    return jax.shard_map(
        local,
        mesh=mesh,
        in_specs=placed,
        out_specs=(P("dp", "weight"), P("dp", "weight"), P("weight", "dp", None, None)),
        check_vma=False,
    )
```

```python
import functools
import math

import jax
import jax.numpy as jnp
from jax import lax
from jax.experimental import pallas as pl
from jax.experimental.pallas import tpu as pltpu
from jax.sharding import PartitionSpec as P

MESH = pl.DeviceIdType.MESH
NY, NZ, NX = 4, 12, 4
F32, BF16 = jnp.float32, jnp.bfloat16


Y_ROWS = 96


def stripe(ref, delta):
    return ref if delta == 0 else ref.at[pl.ds(0, Y_ROWS)]


def rest(ref):
    return ref.at[pl.ds(Y_ROWS, ref.shape[0] - Y_ROWS)]


def rows_of(ref, part, parts):
    size = ref.shape[0] // parts
    return ref.at[pl.ds(part * size, size)]


def mod(a, n):
    return lax.rem(a + n, n)


def hops(delta, side):
    long_way, short_way = NZ // 2, NZ - 1 - NZ // 2
    return long_way if (delta + side) % 2 == 0 else short_way


LONG = NZ // 2


def is_long(delta, side):
    return hops(delta, side) == LONG


def greet(partners):
    barrier = pltpu.get_barrier_semaphore()
    for dp, weight in partners:
        pl.semaphore_signal(barrier, inc=1, device_id=(dp, weight), device_id_type=MESH)

    def wait():
        pl.semaphore_wait(barrier, len(partners))

    return wait


def gather_kernel(own_ref, out_ref, own_sem, y_send, y_recv, z_send, z_recv, r_send, r_recv):
    dp, weight = lax.axis_index("dp"), lax.axis_index("weight")
    j, z = dp // NZ, lax.rem(dp, NZ)
    sides = (mod(z + 1, NZ), mod(z - 1, NZ))
    far = (mod(z + 2, NZ), mod(z - 2, NZ))
    ready = greet(
        [(mod(j + delta, NY) * NZ + z, weight) for delta in range(1, NY)]
        + [(j * NZ + side, weight) for side in sides + far]
    )
    keep = pltpu.make_async_copy(own_ref, out_ref.at[dp], own_sem)
    keep.start()
    ready()

    def send(src, dst, send_sem, recv_sem, device):
        return pltpu.make_async_remote_copy(
            src_ref=src, dst_ref=dst, send_sem=send_sem, recv_sem=recv_sem,
            device_id=(device, weight), device_id_type=MESH,
        )

    def y_copy(delta):
        return send(
            own_ref, out_ref.at[dp], y_send.at[delta - 1], y_recv.at[delta - 1],
            mod(j + delta, NY) * NZ + z,
        )

    def z_copy(side, delta, step):
        held = min(step, LONG - 2)
        back = -held if side == 0 else held
        slot = mod(j - delta, NY) * NZ + mod(z + back, NZ)
        src = own_ref if (delta == 0 and step == 0) else out_ref.at[slot]
        at = (side, delta, step)
        return send(
            stripe(src, delta), stripe(out_ref.at[slot], delta), z_send.at[at], z_recv.at[at],
            j * NZ + (far if step == LONG - 1 else sides)[side],
        )

    def rest_copy(delta, side, step):
        back = -step - 1 if side == 0 else step + 1
        slot = j * NZ + mod(z + back, NZ)
        at = (delta - 1, side, step)
        return send(
            rest(out_ref.at[slot]), rest(out_ref.at[slot]), r_send.at[at], r_recv.at[at],
            mod(j + delta, NY) * NZ + z,
        )

    started = []

    def go(copy):
        copy.start()
        started.append(copy)

    def z_step(delta, step):
        for side in range(2):
            if step > hops(delta, side):
                continue
            if step > 0:
                z_copy(side, delta, step - 1).wait_recv()
            if step < min(hops(delta, side), LONG - 1):
                go(z_copy(side, delta, step))
            if step == LONG - 2 and is_long(delta, side):
                go(z_copy(side, delta, LONG - 1))
        for side in range(2):
            if delta == 0 and 0 < step <= hops(0, side):
                for other in range(1, NY):
                    go(rest_copy(other, side, step - 1))

    z_step(0, 0)
    for delta in range(1, NY):
        go(y_copy(delta))
    for step in range(NZ // 2 + 1):
        z_step(0, step + 1)
        for delta in (1, 3, 2):
            if step == 0:
                y_copy(delta).wait_recv()
            z_step(delta, step)
    for side in range(2):
        for step in range(hops(0, side)):
            for delta in range(1, NY):
                rest_copy(delta, side, step).wait_recv()
    for copy in started:
        copy.wait_send()
    keep.wait()


def gather_blocks(own, slots):
    size = own.shape
    vmem = pl.BlockSpec(memory_space=pltpu.VMEM)
    return pl.pallas_call(
        gather_kernel,
        out_shape=jax.ShapeDtypeStruct((slots,) + size, own.dtype),
        in_specs=[vmem],
        out_specs=vmem,
        scratch_shapes=[
            pltpu.SemaphoreType.DMA,
            pltpu.SemaphoreType.DMA((NY - 1,)),
            pltpu.SemaphoreType.DMA((NY - 1,)),
            pltpu.SemaphoreType.DMA((2, NY, NZ // 2)),
            pltpu.SemaphoreType.DMA((2, NY, NZ // 2)),
            pltpu.SemaphoreType.DMA((NY - 1, 2, NZ // 2)),
            pltpu.SemaphoreType.DMA((NY - 1, 2, NZ // 2)),
        ],
        compiler_params=pltpu.CompilerParams(
            collective_id=0, has_side_effects=True, vmem_limit_bytes=4 << 20
        ),
        cost_estimate=pl.CostEstimate(flops=40_000_000_000, bytes_accessed=60_000_000, transcendentals=0),
        name="gather_blocks",
    )(own)


UNROLL = 24


def local_kernel(
    rows_ref, cols_ref, count_ref, tokens_ref, blocks_ref, cot_ref,
    act_ref, picked_ref, spread_ref, before_ref, last_ref, acc_ref, grad_pre_ref,
):
    slots = blocks_ref.shape[0]
    col_blocks = grad_pre_ref.shape[0]
    count = count_ref[0]
    for row in range(last_ref.shape[0]):
        last_ref[row] = slots
    for slot in range(slots):
        row = rows_ref[0, slot]
        known = last_ref[row]
        before_ref[slot] = known
        last_ref[row] = jnp.where(slot < count, slot, known)
    acc_ref[...] = jnp.zeros_like(acc_ref)

    def forward(group, carry):
        for at in range(UNROLL):
            slot = group * UNROLL + at
            live = slot < count
            col = jnp.where(live, cols_ref[0, slot], col_blocks)
            picked = tokens_ref[:, pl.ds(pl.multiple_of(rows_ref[0, slot] * 128, 128), 128)]
            picked_ref[slot] = picked * live.astype(BF16)
            acc_ref[col] += jnp.dot(picked, blocks_ref[slot], preferred_element_type=F32)
        return carry

    lax.fori_loop(0, slots // UNROLL, forward, 0)
    for col in range(col_blocks):
        here = slice(col * 128, col * 128 + 128)
        preact = acc_ref[col]
        gate = jax.nn.sigmoid(preact)
        act_ref[:, here] = (preact * gate).astype(BF16)
        grad_pre_ref[col] = (
            cot_ref[:, here].astype(F32) * gate * (1.0 + preact * (1.0 - gate))
        ).astype(BF16)

    for slot in range(slots):
        spread_ref[slot] = grad_pre_ref[cols_ref[0, slot]]


def local_work(rows, cols, count, tokens, blocks, cot):
    tok, feat = tokens.shape
    panel = cot.shape[1]
    slots = blocks.shape[0]
    smem = pl.BlockSpec(memory_space=pltpu.SMEM)
    vmem = pl.BlockSpec(memory_space=pltpu.VMEM)
    return pl.pallas_call(
        local_kernel,
        out_shape=(
            jax.ShapeDtypeStruct((tok, panel), BF16),
            jax.ShapeDtypeStruct((slots, tok, 128), BF16),
            jax.ShapeDtypeStruct((slots, tok, 128), BF16),
            jax.ShapeDtypeStruct((slots,), jnp.int32),
            jax.ShapeDtypeStruct((feat // 128,), jnp.int32),
        ),
        in_specs=[smem, smem, smem, vmem, vmem, vmem],
        out_specs=(vmem, vmem, vmem, smem, smem),
        scratch_shapes=[
            pltpu.VMEM((panel // 128 + 1, tok, 128), F32),
            pltpu.VMEM((panel // 128, tok, 128), BF16),
        ],
        compiler_params=pltpu.CompilerParams(vmem_limit_bytes=32 << 20),
        name="local_work",
    )(rows, cols, count, tokens, blocks, cot)


def reduce_kernel(
    scale, before_ref, last_ref, picked_ref, spread_ref, blocks_ref, in_grad_ref, block_grad_ref,
    terms, back_ref, z_buf, z_own, z_first, r_buf, r_out, y_buf, y_out, c_buf, x_sum, x_buf, h_out, h_buf,
    z_send, z_recv, r_send, r_recv, y_send, y_recv, c_send, c_recv, x_send, x_recv,
    h_send, h_recv,
):
    dp, weight = lax.axis_index("dp"), lax.axis_index("weight")
    j, z = dp // NZ, lax.rem(dp, NZ)
    x, h, core = weight // 4, lax.rem(weight // 2, 2), lax.rem(weight, 2)
    sides = (mod(z + 1, NZ), mod(z - 1, NZ))
    far = (mod(z + 2, NZ), mod(z - 2, NZ))
    x_sides = (mod(x + 1, NX), mod(x - 1, NX))
    sibling = weight + 1 - 2 * core
    x_weight = [(side * 2 + h) * 2 + core for side in x_sides]
    h_weight = (x * 2 + 1 - h) * 2 + core
    ready = greet(
        [(mod(j + delta, NY) * NZ + z, weight) for delta in range(1, NY)]
        + [(j * NZ + side, weight) for side in sides + far]
        + [(dp, sibling)]
        + [(dp, side) for side in x_weight]
        + [(dp, h_weight)]
    )
    started = []

    def go(copy):
        copy.start()
        started.append(copy)

    def send(src, dst, send_sem, recv_sem, device):
        return pltpu.make_async_remote_copy(
            src_ref=src, dst_ref=dst, send_sem=send_sem, recv_sem=recv_sem,
            device_id=device, device_id_type=MESH,
        )

    def offset(side, delta, step):
        ahead = hops(delta, side) - step
        return ahead if side == 0 else NZ - ahead

    def block_grad(delta, off):
        slot = mod(j + delta, NY) * NZ + mod(z + off, NZ)
        z_own[delta, off] = lax.dot_general(
            picked_ref[slot], spread_ref[slot], (((0,), (0,)), ((), ())),
            preferred_element_type=F32,
        )
        if delta > 0 and off > 0:
            r_out[delta - 1, off] = z_own[delta, off, Y_ROWS:].astype(BF16)

    def rest_copy(delta, off):
        at = (delta - 1, off)
        return send(
            r_out.at[at], r_buf.at[at], r_send.at[at], r_recv.at[at],
            (mod(j + delta, NY) * NZ + z, weight),
        )

    def z_copy(side, delta, step):
        if step == 0 or (step == 1 and is_long(delta, side)):
            src = z_first.at[side, delta, step]
        else:
            src = z_buf.at[side, delta, step - 1]
        at = (side, delta, step)
        target = far if step == 0 and is_long(delta, side) else sides
        return send(
            stripe(src, delta), stripe(z_buf.at[at], delta), z_send.at[at], z_recv.at[at],
            (j * NZ + target[side], weight),
        )

    def z_add(side, delta, step):
        off = offset(side, delta, step)
        if delta == 0:
            for other in range(1, NY):
                rest_copy(other, off).wait_recv()
                z_own[0, off, Y_ROWS:] += r_buf[other - 1, off].astype(F32)
        many = 128 if delta == 0 else Y_ROWS
        own = z_own[delta, off, :many]
        if step == 0 or (step == 1 and is_long(delta, side)):
            z_first[side, delta, step, :many] = own.astype(BF16)
        else:
            if step == 2 and is_long(delta, side):
                z_copy(side, delta, 0).wait_recv()
                own += z_buf[side, delta, 0, :many].astype(F32)
            z_copy(side, delta, step - 1).wait_recv()
            z_buf[side, delta, step - 1, :many] = (
                z_buf[side, delta, step - 1, :many].astype(F32) + own
            ).astype(BF16)
        go(z_copy(side, delta, step))

    def z_step(turn, deltas):
        for delta in deltas:
            for side in range(2):
                if turn == 0:
                    z_add(side, delta, 0)
                if is_long(delta, side):
                    z_add(side, delta, turn + 1)
                elif turn > 0:
                    z_add(side, delta, turn)

    def back_terms():
        slots = blocks_ref.shape[0]
        terms[slots] = jnp.zeros_like(terms[slots])
        for slot in range(slots):
            terms[slot] = terms[before_ref[slot]] + lax.dot_general(
                spread_ref[slot], blocks_ref[slot], (((1,), (1,)), ((), ())),
                preferred_element_type=F32,
            )
        wide = back_ref.shape[2] // 128
        for row in range(last_ref.shape[0]):
            at = (row % wide) * 128
            back_ref[row // wide, :, at:at + 128] = terms[last_ref[row]].astype(BF16)

    def owner(dx, half, which):
        return (mod(x + dx, NX) * 2 + mod(h + half, 2)) * 2 + which

    def c_copy(dx, half):
        return send(
            back_ref.at[owner(dx, half, 1 - core)], c_buf.at[dx, half],
            c_send.at[dx, half], c_recv.at[dx, half], (dp, sibling),
        )

    def c_sum(dx, half):
        c_copy(dx, half).wait_recv()
        return c_buf[dx, half].astype(F32) + back_ref[owner(dx, half, core)].astype(F32)

    def x_copy(side, what, part=0, parts=1):
        at = (side, what, part)
        return send(
            rows_of(x_sum.at[side, what], part, parts), rows_of(x_buf.at[side, what], part, parts),
            x_send.at[at], x_recv.at[at], (dp, x_weight[side]),
        )

    def h_copy(part):
        return send(
            rows_of(h_out, part, 2), rows_of(h_buf, part, 2), h_send.at[part], h_recv.at[part],
            (dp, h_weight),
        )

    half_rows = h_out.shape[0] // 2
    halves = [(part, slice(part * half_rows, part * half_rows + half_rows)) for part in range(2)]

    others, own = (2, 1, 3), (0,)
    middle = NZ // 2
    offs = sorted(range(NZ), key=lambda off: (abs(off - middle), off > middle))
    first = offs[:3]
    for off in first:
        for delta in range(NY):
            block_grad(delta, off)
    ready()
    for off in first:
        for delta in range(1, NY):
            go(rest_copy(delta, off))
    z_step(0, others)
    back_terms()
    for dx, half in [(2, 1), (3, 1), (2, 0), (1, 1), (3, 0), (1, 0), (0, 1), (0, 0)]:
        go(c_copy(dx, half))
    for off in offs[3:]:
        for delta in range(NY):
            block_grad(delta, off)
        if off > 0:
            for delta in range(1, NY):
                go(rest_copy(delta, off))
    x_sum[0, 0] = c_sum(2, 1).astype(BF16)
    for part in range(2):
        go(x_copy(0, 0, part, 2))
    z_step(1, others)
    x_sum[1, 1] = c_sum(3, 1).astype(BF16)
    go(x_copy(1, 1))
    z_step(0, own)
    x_sum[1, 0] = c_sum(2, 0).astype(BF16)
    go(x_copy(1, 0))
    own_right, own_left = c_sum(1, 1), c_sum(3, 0)
    z_step(2, others)
    z_step(1, own)
    for part, here in halves:
        x_copy(0, 0, part, 2).wait_recv()
        x_sum[0, 2, here] = (own_right[here] + x_buf[0, 0, here].astype(F32)).astype(BF16)
        go(x_copy(0, 2, part, 2))
    x_sum[0, 1] = c_sum(1, 0).astype(BF16)
    go(x_copy(0, 1))
    total = c_sum(0, 1)
    z_step(3, others)
    z_step(2, own)
    x_copy(1, 0).wait_recv()
    x_sum[1, 2] = (own_left + x_buf[1, 0].astype(F32)).astype(BF16)
    go(x_copy(1, 2))
    x_copy(1, 1).wait_recv()
    total += x_buf[1, 1].astype(F32)
    for part, here in halves:
        x_copy(0, 2, part, 2).wait_recv()
        h_out[here] = (total[here] + x_buf[0, 2, here].astype(F32)).astype(BF16)
        go(h_copy(part))
    z_step(4, others)
    z_step(3, own)

    def z_total(delta):
        many = 128 if delta == 0 else Y_ROWS
        for side in range(2):
            last = hops(delta, side) - 1
            z_copy(side, delta, last).wait_recv()
            z_own[delta, 0, :many] += z_buf[side, delta, last, :many].astype(F32)
        return z_own[delta, 0]

    def y_copy(delta):
        return send(
            y_out.at[delta - 1], y_buf.at[delta - 1], y_send.at[delta - 1], y_recv.at[delta - 1],
            (mod(j + delta, NY) * NZ + z, weight),
        )

    for delta in others:
        y_out[delta - 1] = z_total(delta).astype(BF16)
        go(y_copy(delta))
    z_step(4, own)
    grad = z_total(0)
    total = c_sum(0, 0)
    x_copy(0, 1).wait_recv()
    total += x_buf[0, 1].astype(F32)
    x_copy(1, 2).wait_recv()
    total += x_buf[1, 2].astype(F32)
    for delta in (1, 3, 2):
        y_copy(delta).wait_recv()
        grad += y_buf[delta - 1].astype(F32)
    block_grad_ref[...] = grad * scale
    for part, here in halves:
        h_copy(part).wait_recv()
        in_grad_ref[here] = (total[here] + h_buf[here].astype(F32)).astype(BF16)
    for copy in started:
        copy.wait_send()


def reduce_all(before, last, picked, spread, blocks, owners, scale):
    slots, tok = picked.shape[:2]
    vmem, smem = pl.BlockSpec(memory_space=pltpu.VMEM), pl.BlockSpec(memory_space=pltpu.SMEM)
    part, block = (tok, last.shape[0] * 128 // owners), (128, 128)
    dma = pltpu.SemaphoreType.DMA
    return pl.pallas_call(
        functools.partial(reduce_kernel, scale),
        out_shape=(
            jax.ShapeDtypeStruct(part, BF16),
            jax.ShapeDtypeStruct(block, F32),
        ),
        in_specs=[smem, smem, vmem, vmem, vmem],
        out_specs=(vmem, vmem),
        scratch_shapes=[
            pltpu.VMEM((slots + 1, tok, 128), F32),
            pltpu.VMEM((owners,) + part, BF16),
            pltpu.VMEM((2, NY, NZ // 2) + block, BF16),
            pltpu.VMEM((NY, NZ) + block, F32),
            pltpu.VMEM((2, NY, 2) + block, BF16),
            pltpu.VMEM((NY - 1, NZ, 128 - Y_ROWS, 128), BF16),
            pltpu.VMEM((NY - 1, NZ, 128 - Y_ROWS, 128), BF16),
            pltpu.VMEM((NY - 1,) + block, BF16),
            pltpu.VMEM((NY - 1,) + block, BF16),
            pltpu.VMEM((NX, 2) + part, BF16),
            pltpu.VMEM((2, 3) + part, BF16),
            pltpu.VMEM((2, 3) + part, BF16),
            pltpu.VMEM(part, BF16),
            pltpu.VMEM(part, BF16),
            dma((2, NY, NZ // 2)),
            dma((2, NY, NZ // 2)),
            dma((NY - 1, NZ)),
            dma((NY - 1, NZ)),
            dma((NY - 1,)),
            dma((NY - 1,)),
            dma((NX, 2)),
            dma((NX, 2)),
            dma((2, 3, 2)),
            dma((2, 3, 2)),
            dma((2,)),
            dma((2,)),
        ],
        compiler_params=pltpu.CompilerParams(
            collective_id=1, has_side_effects=True, vmem_limit_bytes=32 << 20
        ),
        name="reduce_all",
    )(before, last, picked, spread, blocks)


def local(tokens, block_values, block_rows, block_cols, block_counts, cotangent):
    owners = lax.axis_size("weight")
    blocks = gather_blocks(block_values[0, 0], block_rows.shape[1])
    rows, cols, count = block_rows, block_cols, block_counts
    activated, picked, spread, before, last = local_work(
        rows, cols, count, tokens, blocks, cotangent
    )
    scale = 1.0 / math.sqrt(tokens.shape[0] * lax.axis_size("dp"))
    input_grad, block_grad = reduce_all(before, last, picked, spread, blocks, owners, scale)
    return (activated, input_grad, block_grad.reshape(block_values.shape))


def solution(mesh):
    placed = (
        P("dp", None),
        P("weight", "dp", None, None),
        P("weight", None),
        P("weight", None),
        P("weight"),
        P("dp", "weight"),
    )
    return jax.shard_map(
        local,
        mesh=mesh,
        in_specs=placed,
        out_specs=(P("dp", "weight"), P("dp", "weight"), P("weight", "dp", None, None)),
        check_vma=False,
    )
```
